256 devices in a mesh: adapter: 32 (over z, y), tensor: 8 (over x, core).
Axes of the slice: x: 4, y: 4, z: 8, core: 2. Of those that a mesh axis runs over, the one named last changes fastest.
Arguments:
- queries: bfloat16 [4096, 4, 4096], P('adapter', None, 'tensor'), may hold values from -160 to 160
- shared_prefix_cache: bfloat16 [2, 64, 2048, 1024], P(None, 'adapter', None, 'tensor'), may hold values from -6 to 6
- rollout_suffix_cache: bfloat16 [2, 4096, 32, 1024], P(None, 'adapter', None, 'tensor'), may hold values from -9 to 9
- fresh_key_value: bfloat16 [2, 4096, 4, 1024], P(None, 'adapter', None, 'tensor'), may hold values from -9 to 9
- rollout_prefix_index: int32 [4096], P('adapter'), may hold values from 0 to 63, as said below
- rollout_suffix_length: int32 [4096], P('adapter'), may hold values from 1 to 32, as said below
- rollout_adapter_index: int32 [4096, 1], P('adapter'), may hold values from 0 to 127; in each aligned block of 128 rows (0 to 127, 128 to 255, ...) at most 5 rows name the same one
- output_projection_weight: bfloat16 [4096, 4096], P('tensor'), may hold values from -0.75 to 0.75
- adapter_shrink_weight: bfloat16 [128, 64, 4096], P('adapter', None, 'tensor'), may hold values from -0.75 to 0.75
- adapter_expand_weight: bfloat16 [128, 64, 4096], P('adapter', None, 'tensor'), may hold values from -0.75 to 0.75
Outputs:
- mixed: bfloat16 [4096, 4, 4096], P('adapter', None, 'tensor')
The draws below stay inside these ranges and needn't reach their ends.
Inputs may be any that keep to these rules, and one draw needn't show every extreme that they name: rollout_prefix_index[r] // 2 == r // 128: a rollout's prefix is held with it, and the rollouts of one device name each of its 2 prefixes. `rollout_suffix_length`: among the rollouts of one device some has generated 32 tokens. `rollout_adapter_index`: within the rollouts of one device (aligned blocks of 128 rows) no adapter is named more than 5 times, a bound that some block reaches.
All inputs are finite; a program needn't handle non-finite values.
Results may differ from the reference program's by a relative error of at most 0.015.
Values may be sent and summed in bfloat16 or wider, within the bound.
A program may use at most 128 MiB of HBM per device.

```python
import math
from functools import partial
import jax
import jax.numpy as jnp
import numpy as np
from jax import lax

HEAD_SIZE = 128
QUERY_HEADS = 32
KVH = 8
OUTPUT_FEATURES = 4096
ADAPTER_RANK = 64
MOST = 5
STEPS = 4
PLEN = 2048
SUF = 32
PREF_DEV = 2
ROLL_DEV = 128
ROLLOUTS = 4096
PREFIXES = 64
ADAPTER_COUNT = 128
N_TENSOR = 8


def prefix_ids(key):
    first_key, second_key = jax.random.split(jax.random.fold_in(key, 101))
    block_count = ROLLOUTS // ROLL_DEV
    inner_index = (jnp.arange(ROLLOUTS, dtype=jnp.int32) % ROLL_DEV).reshape(block_count, ROLL_DEV)
    drawn_scores = jax.random.randint(first_key, (block_count, ROLL_DEV), 0, 1 << 20, dtype=jnp.int32) * ROLL_DEV + inner_index
    rank_order = jnp.argsort(jnp.argsort(drawn_scores, axis=1), axis=1).reshape(ROLLOUTS).astype(jnp.int32)
    picked = jax.random.randint(second_key, (ROLLOUTS,), 0, PREF_DEV, dtype=jnp.int32)
    local_index = jnp.where(rank_order < PREF_DEV, rank_order, picked)
    return jnp.arange(ROLLOUTS, dtype=jnp.int32) // ROLL_DEV * PREF_DEV + local_index


def prefix_cache(key):
    cache_key = jax.random.fold_in(key, 202)
    grid_shape = (2, PREFIXES, PLEN, KVH * HEAD_SIZE)
    cache_draw = jnp.clip(jax.random.normal(cache_key, grid_shape, jnp.float32), -6.0, 6.0)
    return cache_draw


def draw_shared_prefix_cache(key, part):
    return prefix_cache(key).astype(jnp.bfloat16)


def draw_rollout_prefix_index(key, part):
    return prefix_ids(key)


def draw_rollout_suffix_length(key, part):
    first_key, second_key = jax.random.split(jax.random.fold_in(key, 404))
    drawn_lengths = jax.random.randint(first_key, (ROLLOUTS,), 1, SUF + 1, dtype=jnp.int32)
    block_count = ROLLOUTS // ROLL_DEV
    picked = jax.random.randint(second_key, (block_count,), 0, ROLL_DEV, dtype=jnp.int32)
    longest = jnp.arange(ROLLOUTS, dtype=jnp.int32) % ROLL_DEV == jnp.repeat(picked, ROLL_DEV)
    return jnp.where(longest, SUF, drawn_lengths).astype(jnp.int32)


def draw_queries(key, part):
    query_key = jax.random.fold_in(key, 303)
    grid_shape = (ROLLOUTS, STEPS, QUERY_HEADS * HEAD_SIZE)
    drawn = jnp.clip(2.0 * jax.random.normal(query_key, grid_shape, jnp.float32), -12.0, 12.0)
    return drawn.astype(jnp.bfloat16)


def block_levels(own_key, dims, cuts, least, top_value):
    def one(dim, shards_of):
        draws = jax.random.uniform(jax.random.fold_in(jax.random.fold_in(own_key, 6), dim), (shards_of,), jnp.float32, least / len(cuts), top_value / len(cuts))
        return jnp.repeat(jnp.exp(draws), dims[dim] // shards_of).reshape((-1,) + (1,) * (len(dims) - dim - 1))

    loudness = one(*cuts[0])
    for cut in cuts[1:]:
        loudness = loudness * one(*cut)
    return loudness


def routed_block(stream_key, own, number, rows, amount, top, most, skew):
    ranking = jax.random.permutation(stream_key, amount)
    packed, common = load_shares(amount, rows * top, most, skew, True), load_shares(amount, rows * top, most, skew, False)
    places = jnp.arange(amount)

    def named(lengths, turn):
        used = int((lengths > 0).sum())
        fixed = max(1, used // 4)
        shifted = fixed + (places - fixed + turn * (used - fixed)) % max(1, amount - fixed)
        return jnp.zeros((amount,), jnp.int32).at[ranking[jnp.where(places < fixed, places, shifted)]].set(jnp.asarray(lengths, jnp.int32))

    lengths = jnp.where(number % 4 == 0, named(packed, number // 4), named(common, number - number // 4 - 1))
    mixed = jax.random.permutation(jax.random.fold_in(own, 3), amount)
    source_of, taker = mixed[0:amount // 2 * 2:2], mixed[1:amount // 2 * 2:2]
    margin = jnp.minimum(lengths[source_of] - 1, most - lengths[taker]) // 2
    margin = jnp.where((source_of == ranking[0]) | (taker == ranking[0]) | (lengths[taker] == 0), 0, jnp.maximum(margin, 0))
    shifted = jax.random.randint(jax.random.fold_in(own, 4), (amount // 2,), 0, 1 << 20) % (margin + 1)
    lengths = lengths.at[source_of].add(-shifted).at[taker].add(shifted)
    labels = jnp.searchsorted(jnp.cumsum(lengths), jnp.arange(rows * top), side="right").astype(jnp.int32)
    table = labels.reshape(top, rows).T
    table = table[jax.random.permutation(jax.random.fold_in(own, 1), rows)]
    turn = jax.random.randint(jax.random.fold_in(own, 2), (rows, 1), 0, top)
    return jnp.take_along_axis(table, (jnp.arange(top)[None, :] + turn) % top, axis=1)


def load_shares(amount, total, reach, lean, full):
    portions = [(1 << 20) // math.isqrt(rank ** lean) + 1 for rank in range(1, amount + 1)]
    largest = reach if full else min(reach, max(-(-total // amount), total * portions[0] // sum(portions)))
    least = 1 if total - largest >= amount - 1 else 0
    given, surplus = [largest] + [least] * (amount - 1), total - largest - least * (amount - 1)
    while surplus > 0:
        movable = [i for i in range(1, amount) if given[i] < largest] or [i for i in range(1, amount) if given[i] < reach]
        mass, left = sum([portions[i] for i in movable]), surplus
        for i in movable:
            extra = min(reach - given[i], max(1, left * portions[i] // mass), surplus)
            given[i] = given[i] + extra
            surplus = surplus - extra
    return np.array(given)


def noise(stream_key, dims, width, bound, cuts=(), held_as=jnp.bfloat16):
    array = width * jax.random.normal(stream_key, dims, jnp.float32)
    if cuts:
        array = array * block_levels(stream_key, dims, cuts, -0.22, 0.18)
    return jnp.clip(array, -bound, bound).astype(held_as)


def setup_inputs(seed: int = 0) -> dict:
    streams_of = jax.random.split(jax.random.key(seed), 11)
    queries = draw_queries(jax.random.fold_in(streams_of[10], 71), 0)
    shared_prefix_cache = draw_shared_prefix_cache(jax.random.fold_in(streams_of[10], 71), 0)
    rollout_suffix_cache = noise(streams_of[2], (2, ROLLOUTS, SUF, KVH * HEAD_SIZE), 1.5, 9.0, ((1, 32), (3, 8)))
    fresh_key_value = noise(streams_of[3], (2, ROLLOUTS, STEPS, KVH * HEAD_SIZE), 1.5, 9.0, ((1, 32), (3, 8)))
    rollout_prefix_index = draw_rollout_prefix_index(jax.random.fold_in(streams_of[10], 71), 0)
    rollout_suffix_length = draw_rollout_suffix_length(jax.random.fold_in(streams_of[10], 71), 0)
    rollout_adapter_index_keys = jax.random.split(jax.random.fold_in(streams_of[6], 1), ROLLOUTS // ROLL_DEV)
    rollout_adapter_index_turns = jax.random.permutation(jax.random.fold_in(streams_of[6], 3), ROLLOUTS // ROLL_DEV)
    rollout_adapter_index = jax.vmap(lambda own, number: routed_block(jax.random.fold_in(streams_of[6], 2), own, number, ROLL_DEV, ADAPTER_COUNT, 1, MOST, 2))(rollout_adapter_index_keys, rollout_adapter_index_turns).reshape((ROLLOUTS, 1))
    output_projection_weight = noise(streams_of[7], (QUERY_HEADS * HEAD_SIZE, OUTPUT_FEATURES), (QUERY_HEADS * HEAD_SIZE // 64) ** -0.5, 0.75, ((0, 8),))
    adapter_shrink_weight = noise(streams_of[8], (ADAPTER_COUNT, ADAPTER_RANK, QUERY_HEADS * HEAD_SIZE), (QUERY_HEADS * HEAD_SIZE // 64) ** -0.5, 0.75, ((0, 32), (2, 8)))
    adapter_expand_weight = noise(streams_of[9], (ADAPTER_COUNT, ADAPTER_RANK, OUTPUT_FEATURES), ADAPTER_RANK ** -0.5, 0.75, ((0, 32), (2, 8)))
    return {"queries": queries, "shared_prefix_cache": shared_prefix_cache, "rollout_suffix_cache": rollout_suffix_cache, "fresh_key_value": fresh_key_value, "rollout_prefix_index": rollout_prefix_index, "rollout_suffix_length": rollout_suffix_length, "rollout_adapter_index": rollout_adapter_index, "output_projection_weight": output_projection_weight, "adapter_shrink_weight": adapter_shrink_weight, "adapter_expand_weight": adapter_expand_weight}


def attend_rollout(shared_prefix_cache, query_rows, suffix_part, fresh_part, prefix_index, length):
    chosen = lax.dynamic_index_in_dim(shared_prefix_cache, prefix_index, axis=1, keepdims=False)
    joined = jnp.concatenate([chosen, suffix_part, fresh_part], axis=1)
    total_keys = PLEN + SUF + STEPS
    key_rows = joined[0].astype(jnp.float32).reshape(total_keys, KVH, HEAD_SIZE)
    values = joined[1].astype(jnp.float32).reshape(total_keys, KVH, HEAD_SIZE)
    grouped = query_rows.astype(jnp.float32).reshape(STEPS, KVH, QUERY_HEADS // KVH, HEAD_SIZE)
    scores = jnp.einsum("skgd,tkd->skgt", grouped, key_rows) * (HEAD_SIZE ** -0.5)
    position = jnp.arange(total_keys)[None, :]
    step_ids = jnp.arange(STEPS)[:, None]
    visible = (position < PLEN) | ((position < PLEN + SUF) & (position - PLEN < length)) | ((position >= PLEN + SUF) & (position - PLEN - SUF <= step_ids))
    scores = jnp.where(visible[:, None, None, :], scores, -jnp.inf)
    row_top = jnp.max(scores, axis=-1, keepdims=True)
    exponent = jnp.exp(scores - row_top)
    weights = (exponent / jnp.sum(exponent, axis=-1, keepdims=True)).astype(jnp.bfloat16)
    attention_output = jnp.einsum("skgt,tkd->skgd", weights.astype(jnp.float32), values)
    return attention_output.reshape(STEPS, QUERY_HEADS * HEAD_SIZE).astype(jnp.bfloat16)


def apply_rollout_adapter(adapter_shrink_weight, adapter_expand_weight, bundle_member):
    rows_here, identity_value = bundle_member
    shrink_table = lax.dynamic_index_in_dim(adapter_shrink_weight, identity_value, axis=0, keepdims=False)
    expand_table = lax.dynamic_index_in_dim(adapter_expand_weight, identity_value, axis=0, keepdims=False)
    rank_features = jnp.dot(rows_here, shrink_table.T, preferred_element_type=jnp.float32).astype(jnp.bfloat16)
    return jnp.dot(rank_features, expand_table, preferred_element_type=jnp.float32).astype(jnp.bfloat16)


def reference(queries, shared_prefix_cache, rollout_suffix_cache, fresh_key_value, rollout_prefix_index, rollout_suffix_length, rollout_adapter_index, output_projection_weight, adapter_shrink_weight, adapter_expand_weight):
    bundle = 4
    groups = ROLLOUTS // bundle
    suffix_rows = jnp.moveaxis(rollout_suffix_cache, 1, 0).reshape(groups, bundle, 2, SUF, KVH * HEAD_SIZE)
    fresh_rows = jnp.moveaxis(fresh_key_value, 1, 0).reshape(groups, bundle, 2, STEPS, KVH * HEAD_SIZE)

    def attend_bundle(bundle_member):
        query_part, suffix_part, fresh_part, prefix_part, length_part = bundle_member
        return jax.vmap(partial(attend_rollout, shared_prefix_cache))(query_part, suffix_part, fresh_part, prefix_part, length_part)

    attention_output = lax.map(attend_bundle, (queries.reshape(groups, bundle, STEPS, QUERY_HEADS * HEAD_SIZE), suffix_rows, fresh_rows, rollout_prefix_index.reshape(groups, bundle), rollout_suffix_length.reshape(groups, bundle)))
    attention_output = attention_output.reshape(ROLLOUTS, STEPS, QUERY_HEADS * HEAD_SIZE)
    flat_rows = attention_output.reshape(ROLLOUTS * STEPS, QUERY_HEADS * HEAD_SIZE)
    group_width = QUERY_HEADS * HEAD_SIZE // N_TENSOR
    base_sum = jnp.zeros((ROLLOUTS * STEPS, OUTPUT_FEATURES), jnp.float32)
    for group_index in range(N_TENSOR):
        lower = group_index * group_width
        partial_sum = jnp.dot(flat_rows[:, lower:lower + group_width], output_projection_weight[lower:lower + group_width], preferred_element_type=jnp.float32)
        rounded = lax.optimization_barrier(partial_sum.astype(jnp.bfloat16))
        base_sum = base_sum + rounded.astype(jnp.float32)
    adapter_correction = lax.map(partial(apply_rollout_adapter, adapter_shrink_weight, adapter_expand_weight), (attention_output, rollout_adapter_index[:, 0]))
    mixed = base_sum.reshape(ROLLOUTS, STEPS, OUTPUT_FEATURES) + adapter_correction.astype(jnp.float32)
    return mixed.astype(jnp.bfloat16)
```

```python
import functools, math
import jax
import jax.numpy as jnp
from jax import lax
from jax.experimental import pallas as pl
from jax.experimental.pallas import tpu as pltpu
from jax.sharding import PartitionSpec as P

HEAD = 128
NT = (((1,), (1,)), ((), ()))
F32 = jnp.float32
BF = jnp.bfloat16
MOST = 5


def row_columns(row_ref):
    values = row_ref[...].astype(F32).astype(BF)
    pick = lax.broadcasted_iota(jnp.int32, (512, 128), 0) // 4 == lax.broadcasted_iota(
        jnp.int32, (512, 128), 1
    )
    spread = jnp.where(pick, jnp.broadcast_to(values.astype(F32), (512, 128)), 0.0).astype(BF)
    return jnp.dot(spread, jnp.ones((128, 128), BF), preferred_element_type=F32)


def attend_chunk(base, q_ref, kp, vp, suf, fresh, pcol, lcol, out_ref):
    factor = (HEAD ** -0.5) * math.log2(math.e)
    subs = []
    for sub in range(2):
        row = base + sub * 32
        for h in range(4):
            subs.append(q_ref[row // 4 : row // 4 + 8, :, h * HEAD : (h + 1) * HEAD].reshape(32, HEAD))
    q = jnp.concatenate(subs, axis=0)
    pc = jnp.concatenate(
        [pcol[base + sub * 32 : base + sub * 32 + 32, :] for sub in range(2) for h in range(4)], axis=0
    )
    second = pc > 0.5
    zero = jnp.zeros_like(q)
    wide = jnp.concatenate([jnp.where(second, zero, q), jnp.where(second, q, zero)], axis=1)
    scores = lax.dot_general(wide, kp[...], NT, preferred_element_type=F32)
    top = jnp.max(scores, axis=1, keepdims=True)
    rows_i = lax.broadcasted_iota(jnp.int32, (128, 256), 0)
    keys_i = lax.broadcasted_iota(jnp.int32, (128, 256), 1)
    same = (rows_i % 32) // 4 == keys_i // 32
    kpos = (keys_i % 32).astype(F32)
    rows_f = lax.broadcasted_iota(jnp.int32, (128, 32), 0)
    keys_f = lax.broadcasted_iota(jnp.int32, (128, 32), 1)
    fmask = ((rows_f % 32) // 4 == keys_f // 4) & (keys_f % 4 <= rows_f % 4)
    suf_scores, fresh_scores = [], []
    for sub in range(2):
        r0 = (base + sub * 32) // 4
        qs = q[sub * 128 : (sub + 1) * 128]
        ks = suf[0, r0 * 32 : r0 * 32 + 256, :]
        s = lax.dot_general(qs, ks, NT, preferred_element_type=F32)
        lc = jnp.concatenate([lcol[base + sub * 32 : base + sub * 32 + 32, :]] * 4, axis=0)
        lc = jnp.concatenate([lc, lc], axis=1)
        suf_scores.append(jnp.where(same & (kpos < lc), s, -jnp.inf))
        kf = fresh[0, r0 : r0 + 8].reshape(32, HEAD)
        f = lax.dot_general(qs, kf, NT, preferred_element_type=F32)
        fresh_scores.append(jnp.where(fmask, f, -jnp.inf))
    ssc = jnp.concatenate(suf_scores, axis=0)
    fsc = jnp.concatenate(fresh_scores, axis=0)
    top = jnp.maximum(top, jnp.maximum(jnp.max(ssc, axis=1, keepdims=True), jnp.max(fsc, axis=1, keepdims=True)))
    p = jnp.exp2((scores - top) * factor)
    ps = jnp.exp2((ssc - top) * factor)
    pf = jnp.exp2((fsc - top) * factor)
    total = (
        jnp.sum(p, axis=1, keepdims=True)
        + jnp.sum(ps, axis=1, keepdims=True)
        + jnp.sum(pf, axis=1, keepdims=True)
    )
    both = jnp.dot(p.astype(BF), vp[...], preferred_element_type=F32)
    acc = jnp.where(second, both[:, HEAD:], both[:, :HEAD])
    psb, pfb = ps.astype(BF), pf.astype(BF)
    extra = []
    for sub in range(2):
        r0 = (base + sub * 32) // 4
        vs = suf[1, r0 * 32 : r0 * 32 + 256, :]
        vf = fresh[1, r0 : r0 + 8].reshape(32, HEAD)
        e = jnp.dot(psb[sub * 128 : (sub + 1) * 128], vs, preferred_element_type=F32)
        e = e + jnp.dot(pfb[sub * 128 : (sub + 1) * 128], vf, preferred_element_type=F32)
        extra.append(e)
    acc = acc + jnp.concatenate(extra, axis=0)
    acc = (acc * (1.0 / total)).astype(BF)
    for sub in range(2):
        for h in range(4):
            out_ref[base + sub * 32 : base + sub * 32 + 32, h * HEAD : (h + 1) * HEAD] = acc[
                sub * 128 + h * 32 : sub * 128 + h * 32 + 32
            ]


def attention_kernel(pfx_ref, len_ref, q_ref, prefix, suf, fresh, out_ref, kp, vp, pcol, lcol, sem):
    copies = []
    for which, ref in enumerate((kp, vp)):
        for slot in range(2):
            copies.append(
                pltpu.make_async_copy(
                    prefix.at[which, slot],
                    ref.at[:, slot * HEAD : (slot + 1) * HEAD],
                    sem.at[which * 2 + slot],
                )
            )
    for c in copies:
        c.start()
    pcol[...] = row_columns(pfx_ref)
    lcol[...] = row_columns(len_ref)
    for c in copies:
        c.wait()
    for chunk in range(8):
        attend_chunk(chunk * 64, q_ref, kp, vp, suf, fresh, pcol, lcol, out_ref)


def attention(pfx, lens, queries, prefix, suffix, fresh):
    vm = pl.BlockSpec(memory_space=pltpu.VMEM)
    return pl.pallas_call(
        attention_kernel,
        out_shape=jax.ShapeDtypeStruct((512, 512), BF),
        in_specs=[vm, vm, vm, pl.BlockSpec(memory_space=pl.ANY), vm, vm],
        out_specs=vm,
        scratch_shapes=[
            pltpu.VMEM((2048, 256), BF),
            pltpu.VMEM((2048, 256), BF),
            pltpu.VMEM((512, 128), F32),
            pltpu.VMEM((512, 128), F32),
            pltpu.SemaphoreType.DMA((4,)),
        ],
        compiler_params=pltpu.CompilerParams(vmem_limit_bytes=60 << 20),
        cost_estimate=pl.CostEstimate(flops=5 * 10**9, bytes_accessed=6 * 10**6, transcendentals=4 * 10**6),
    )(pfx, lens, queries, prefix, suffix.reshape(2, 4096, HEAD), fresh)


def head_total(attention_output, output_projection_weight):
    roll_count, step_count, width_here = attention_output.shape
    partial_sum = jnp.dot(
        attention_output.reshape(roll_count * step_count, width_here),
        output_projection_weight,
        preferred_element_type=jnp.float32,
    )
    return lax.psum_scatter(
        partial_sum.astype(jnp.bfloat16), "tensor", scatter_dimension=1, tiled=True
    ).astype(jnp.float32)


def adapter_share(
    attention_output, rollout_adapter_index, adapter_shrink_weight, adapter_expand_weight
):
    roll_count, step_count, width_here = attention_output.shape
    adapter_index = rollout_adapter_index[:, 0]
    axis_count = lax.axis_size("adapter")
    resident_adapters = adapter_shrink_weight.shape[0]
    adapter_total = resident_adapters * axis_count
    output_width = adapter_expand_weight.shape[2]
    one_hot = (
        adapter_index[:, None] == jnp.arange(adapter_total, dtype=jnp.int32)[None, :]
    ).astype(jnp.int32)
    earlier = jnp.cumsum(one_hot, axis=0) - one_hot
    slot_index = adapter_index * MOST + jnp.sum(earlier * one_hot, axis=1)
    payload = attention_output.reshape(roll_count, step_count * width_here)
    outgoing = (
        jnp.zeros((adapter_total * MOST, step_count * width_here), jnp.bfloat16)
        .at[slot_index]
        .set(payload)
    )
    received = lax.all_to_all(
        outgoing.reshape(axis_count, resident_adapters, MOST, step_count * width_here),
        "adapter",
        split_axis=0,
        concat_axis=0,
        tiled=True,
    )
    sources, owned, slots, packed = received.shape
    block_list = received.reshape(sources, owned, slots, step_count, width_here)
    shrink_step = jnp.einsum(
        "jcoxy,cqy->jcoxq", block_list, adapter_shrink_weight, preferred_element_type=jnp.float32
    )
    rank_features = lax.psum(shrink_step.astype(jnp.bfloat16), "tensor")
    expanded = jnp.einsum(
        "jzuvt,ztq->jzuvq", rank_features, adapter_expand_weight, preferred_element_type=jnp.float32
    ).astype(jnp.bfloat16)
    returned = lax.all_to_all(
        expanded.reshape(sources, owned, slots, step_count * output_width),
        "adapter",
        split_axis=0,
        concat_axis=0,
        tiled=True,
    )
    return returned.reshape(adapter_total * MOST, step_count, output_width)[slot_index]


def local(
    queries,
    shared_prefix_cache,
    rollout_suffix_cache,
    fresh_key_value,
    rollout_prefix_index,
    rollout_suffix_length,
    rollout_adapter_index,
    output_projection_weight,
    adapter_shrink_weight,
    adapter_expand_weight,
):
    roll_count, step_count, width_here = queries.shape
    prefix_count = shared_prefix_cache.shape[1]
    local_prefix = rollout_prefix_index - lax.axis_index("adapter") * prefix_count
    attention_output = attention(
        local_prefix.reshape(1, roll_count),
        rollout_suffix_length.reshape(1, roll_count),
        queries,
        shared_prefix_cache,
        rollout_suffix_cache,
        fresh_key_value,
    ).reshape(roll_count, step_count, width_here)
    output_width = adapter_expand_weight.shape[2]
    adapter_correction = adapter_share(
        attention_output, rollout_adapter_index, adapter_shrink_weight, adapter_expand_weight
    )
    base_sum = head_total(attention_output, output_projection_weight)
    mixed = base_sum.reshape(roll_count, step_count, output_width) + adapter_correction.astype(
        jnp.float32
    )
    return mixed.astype(jnp.bfloat16)


def solution(mesh):
    placed = (
        P("adapter", None, "tensor"),
        P(None, "adapter", None, "tensor"),
        P(None, "adapter", None, "tensor"),
        P(None, "adapter", None, "tensor"),
        P("adapter"),
        P("adapter"),
        P("adapter", None),
        P("tensor", None),
        P("adapter", None, "tensor"),
        P("adapter", None, "tensor"),
    )
    return jax.shard_map(
        local, mesh=mesh, in_specs=placed, out_specs=P("adapter", None, "tensor"), check_vma=False
    )
```

```python
import math
import jax
import jax.numpy as jnp
from jax import lax
from jax.experimental import pallas as pl
from jax.experimental.pallas import tpu as pltpu
from jax.sharding import PartitionSpec as P

HEAD = 128
NT = (((1,), (1,)), ((), ()))
F32 = jnp.float32
BF = jnp.bfloat16


def row_columns(row_ref):
    values = row_ref[...].astype(F32).astype(BF)
    pick = lax.broadcasted_iota(jnp.int32, (512, 128), 0) // 4 == lax.broadcasted_iota(
        jnp.int32, (512, 128), 1
    )
    spread = jnp.where(pick, jnp.broadcast_to(values.astype(F32), (512, 128)), 0.0).astype(BF)
    return jnp.dot(spread, jnp.ones((128, 128), BF), preferred_element_type=F32)


def attend_chunk(base, q_ref, kp, vp, suf, fresh, pcol, lcol, out_ref):
    factor = (HEAD ** -0.5) * math.log2(math.e)
    subs = []
    for sub in range(2):
        row = base + sub * 32
        for h in range(4):
            subs.append(q_ref[row // 4 : row // 4 + 8, :, h * HEAD : (h + 1) * HEAD].reshape(32, HEAD))
    q = jnp.concatenate(subs, axis=0)
    pc = jnp.concatenate(
        [pcol[base + sub * 32 : base + sub * 32 + 32, :] for sub in range(2) for h in range(4)], axis=0
    )
    second = pc > 0.5
    zero = jnp.zeros_like(q)
    wide = jnp.concatenate([jnp.where(second, zero, q), jnp.where(second, q, zero)], axis=1)
    scores = lax.dot_general(wide, kp[...], NT, preferred_element_type=F32)
    top = jnp.max(scores, axis=1, keepdims=True)
    rows_i = lax.broadcasted_iota(jnp.int32, (128, 256), 0)
    keys_i = lax.broadcasted_iota(jnp.int32, (128, 256), 1)
    same = (rows_i % 32) // 4 == keys_i // 32
    kpos = (keys_i % 32).astype(F32)
    rows_f = lax.broadcasted_iota(jnp.int32, (128, 32), 0)
    keys_f = lax.broadcasted_iota(jnp.int32, (128, 32), 1)
    fmask = ((rows_f % 32) // 4 == keys_f // 4) & (keys_f % 4 <= rows_f % 4)
    suf_scores, fresh_scores = [], []
    for sub in range(2):
        r0 = (base + sub * 32) // 4
        qs = q[sub * 128 : (sub + 1) * 128]
        ks = suf[0, r0 * 32 : r0 * 32 + 256, :]
        s = lax.dot_general(qs, ks, NT, preferred_element_type=F32)
        lc = jnp.concatenate([lcol[base + sub * 32 : base + sub * 32 + 32, :]] * 4, axis=0)
        lc = jnp.concatenate([lc, lc], axis=1)
        suf_scores.append(jnp.where(same & (kpos < lc), s, -jnp.inf))
        kf = fresh[0, r0 : r0 + 8].reshape(32, HEAD)
        f = lax.dot_general(qs, kf, NT, preferred_element_type=F32)
        fresh_scores.append(jnp.where(fmask, f, -jnp.inf))
    ssc = jnp.concatenate(suf_scores, axis=0)
    fsc = jnp.concatenate(fresh_scores, axis=0)
    top = jnp.maximum(top, jnp.maximum(jnp.max(ssc, axis=1, keepdims=True), jnp.max(fsc, axis=1, keepdims=True)))
    p = jnp.exp2((scores - top) * factor)
    ps = jnp.exp2((ssc - top) * factor)
    pf = jnp.exp2((fsc - top) * factor)
    total = (
        jnp.sum(p, axis=1, keepdims=True)
        + jnp.sum(ps, axis=1, keepdims=True)
        + jnp.sum(pf, axis=1, keepdims=True)
    )
    both = jnp.dot(p.astype(BF), vp[...], preferred_element_type=F32)
    acc = jnp.where(second, both[:, HEAD:], both[:, :HEAD])
    psb, pfb = ps.astype(BF), pf.astype(BF)
    extra = []
    for sub in range(2):
        r0 = (base + sub * 32) // 4
        vs = suf[1, r0 * 32 : r0 * 32 + 256, :]
        vf = fresh[1, r0 : r0 + 8].reshape(32, HEAD)
        e = jnp.dot(psb[sub * 128 : (sub + 1) * 128], vs, preferred_element_type=F32)
        e = e + jnp.dot(pfb[sub * 128 : (sub + 1) * 128], vf, preferred_element_type=F32)
        extra.append(e)
    acc = acc + jnp.concatenate(extra, axis=0)
    acc = (acc * (1.0 / total)).astype(BF)
    for sub in range(2):
        for h in range(4):
            out_ref[base + sub * 32 : base + sub * 32 + 32, h * HEAD : (h + 1) * HEAD] = acc[
                sub * 128 + h * 32 : sub * 128 + h * 32 + 32
            ]


NMSG = 256
MESHID = pl.DeviceIdType.MESH


class Net:
    def __init__(self, ssem, rsem):
        self.ssem, self.rsem, self.sent, self.count = ssem, rsem, [], 0

    def copy(self, src, dst, device):
        i = self.count
        self.count += 1
        d = pltpu.make_async_remote_copy(
            src_ref=src,
            dst_ref=dst,
            send_sem=self.ssem.at[i],
            recv_sem=self.rsem.at[i],
            device_id=device,
            device_id_type=MESHID,
        )
        self.sent.append(d)
        return d


def mega_kernel(
    pfx_ref, len_ref, idx_ref, q_ref, prefix, suf, fresh, wo_hbm, a_hbm, b_hbm,
    out_ref,
    kp, vp, pcol, lcol, wo, ag, bg0, bg1, att, fl, fr, fo, part, pr, s1, s2, s3,
    t2l, t2r, f1l, f3r, idn, idc, acc, cp, cr, cs, cf, xs, e0, e1, ol, orr, eR, eL, dl, dr,
    lsem, ssem, rsem,
):
    a, t = lax.axis_index("adapter"), lax.axis_index("tensor")
    z, y, x, c = a // 4, a % 4, t // 2, t % 2
    zr, zl = (((z + 1) % 8) * 4 + y, t), (((z + 7) % 8) * 4 + y, t)
    yr, yl, yo = (z * 4 + (y + 1) % 4, t), (z * 4 + (y + 3) % 4, t), (z * 4 + (y + 2) % 4, t)
    xr, xl, pc = (a, ((x + 1) % 4) * 2 + c), (a, ((x + 3) % 4) * 2 + c), (a, x * 2 + (1 - c))
    peers = [(a, (t + d) % 8) for d in range(1, 8)]
    net = Net(ssem, rsem)

    barrier = pltpu.get_barrier_semaphore()
    everyone = [zr, zl, yr, yl, yo] + peers
    for dev in everyone:
        pl.semaphore_signal(barrier, inc=1, device_id=dev, device_id_type=MESHID)

    loads, nl = {}, 0

    def load(name, src, dst):
        nonlocal nl
        d = pltpu.make_async_copy(src, dst, lsem.at[nl])
        nl += 1
        loads.setdefault(name, []).append(d)
        d.start()

    def loaded(name):
        for d in loads[name]:
            d.wait()

    for which, ref in enumerate((kp, vp)):
        for slot in range(2):
            load("kv", prefix.at[which, slot], ref.at[:, slot * HEAD : (slot + 1) * HEAD])
    load("a", a_hbm, ag.at[0])
    for j in range(8):
        dest = ((x + j % 4) % 4) * 2 + (c + j // 4) % 2
        load("wo", wo_hbm.at[:, pl.ds(pl.multiple_of(dest * 512, 512), 512)], wo.at[j])
    load("b", b_hbm.at[:, 0:256], bg0.at[0])
    load("b", b_hbm.at[:, 256:512], bg1.at[0])

    own = [a_hbm, b_hbm.at[:, 0:256], b_hbm.at[:, 256:512]]
    store = [ag, bg0, bg1]
    last = {(0, 0): 4, (0, 1): 3, (1, 0): 3, (1, 1): 4}
    hops = {}
    for mat in range(3):
        for h in range(2):
            rows = slice(h * 128, h * 128 + 128)
            for way in range(2):
                for k in range(1, last[(way, h)] + 1):
                    here = (8 - (k - 1)) % 8 if way == 0 else k - 1
                    there = (8 - k) % 8 if way == 0 else k
                    src = own[mat].at[rows] if k == 1 else store[mat].at[here, rows]
                    hops[mat, h, way, k] = net.copy(src, store[mat].at[there, rows], zr if way == 0 else zl)

    def z_first(mat):
        for h in range(2):
            for way in range(2):
                hops[mat, h, way, 1].start()

    def z_step(mat, h, k):
        for way in range(2):
            if k <= last[(way, h)]:
                hops[mat, h, way, k].wait_recv()
                if k < last[(way, h)]:
                    hops[mat, h, way, k + 1].start()

    id_msgs = [
        net.copy(idx_ref, idn.at[0], yr),
        net.copy(idx_ref, idn.at[1], yl),
        net.copy(idx_ref, idn.at[2], yo),
    ]
    pl.semaphore_wait(barrier, len(everyone))
    z_first(0)
    for d in id_msgs:
        d.start()

    pcol[...] = row_columns(pfx_ref)
    lcol[...] = row_columns(len_ref)
    idc[0] = row_columns(idx_ref)

    feat = {}
    for m in range(4):
        rows, ha, hb = slice(m * 128, m * 128 + 128), slice(m * 128, m * 128 + 64), slice(m * 128 + 64, m * 128 + 128)
        feat["r", m] = net.copy(att.at[rows], fl.at[rows], yr)
        feat["l", m] = net.copy(att.at[rows], fr.at[rows], yl)
        feat["rr", m] = net.copy(fl.at[ha], fo.at[ha], yr)
        feat["ll", m] = net.copy(fr.at[hb], fo.at[hb], yl)
    base = {}
    for m in range(4):
        rows, ha, hb = slice(m * 128, m * 128 + 128), slice(m * 128, m * 128 + 64), slice(m * 128 + 64, m * 128 + 128)
        base["p", m] = net.copy(part.at[1, :, rows], pr.at[:, rows], pc)
        base["2r", m] = net.copy(s2.at[ha], t2l.at[ha], xr)
        base["2l", m] = net.copy(s2.at[hb], t2r.at[hb], xl)
        base["1r", m] = net.copy(s1.at[rows], f1l.at[rows], xr)
        base["1l", m] = net.copy(s3.at[rows], f3r.at[rows], xl)

    def project(m):
        rows = slice(m * 128, m * 128 + 128)
        here = att[rows, :]
        for j in (4, 5, 6, 7, 2, 1, 3, 0):
            got = jnp.dot(here, wo[j], preferred_element_type=F32)
            part[j // 4, j % 4, rows, :] = got.astype(BF)
            if j == 7:
                base["p", m].start()

    def forward_features(m):
        feat["r", m].wait_recv()
        feat["rr", m].start()
        feat["l", m].wait_recv()
        feat["ll", m].start()

    def paired(dx, rows):
        return part[0, dx, rows, :].astype(F32) + pr[dx, rows, :].astype(F32)

    def base_two(m):
        base["p", m].wait_recv()
        rows = slice(m * 128, m * 128 + 128)
        s2[rows, :] = paired(2, rows).astype(BF)
        base["2r", m].start()
        base["2l", m].start()

    def base_one(m):
        ha, hb = slice(m * 128, m * 128 + 64), slice(m * 128 + 64, m * 128 + 128)
        base["2r", m].wait_recv()
        s1[ha, :] = (paired(1, ha) + t2l[ha, :].astype(F32)).astype(BF)
        s1[hb, :] = paired(1, hb).astype(BF)
        base["1r", m].start()
        base["2l", m].wait_recv()
        s3[ha, :] = paired(3, ha).astype(BF)
        s3[hb, :] = (paired(3, hb) + t2r[hb, :].astype(F32)).astype(BF)
        base["1l", m].start()

    feats = [att, fl, fr, fo]
    low = lax.broadcasted_iota(jnp.int32, (512, 128), 1) < 64
    lowh = lax.broadcasted_iota(jnp.int32, (256, 128), 1) < 64

    def lane_adapter(g):
        first = ((z + g // 2) % 8) * 16 + y * 4 + (g % 2) * 2
        lanes = lax.broadcasted_iota(jnp.int32, (1, 128), 1) // 64
        return (lanes + first).astype(F32)

    def codes(b):
        total = None
        ids = idc[b]
        for d in range(8):
            got = lax.dot_general(feats[b][...], ag[d], NT, preferred_element_type=F32)
            for half in range(2):
                mine = jnp.where(ids == lane_adapter(2 * d + half), got[:, half * 128 : half * 128 + 128], 0.0)
                total = mine if total is None else total + mine
        acc[...] = total
        folded = acc[...] + pltpu.roll(acc[...], 64, 1)
        cp[b] = jnp.where(lowh, folded[:256], folded[256:]).astype(BF)

    scat, gath = {}, {}
    for b in range(4):
        for d in range(1, 8):
            to = (t + d) % 8
            rows = pl.ds(pl.multiple_of(to * 32, 32), 32)
            scat[b, d] = net.copy(cp.at[b, rows], cr.at[b, d], (a, to))
            rows = pl.ds(pl.multiple_of(t * 32, 32), 32)
            gath[b, d] = net.copy(cs.at[b], cf.at[b, rows], (a, to))

    def scatter_codes(b):
        for d in range(1, 8):
            scat[b, d].start()

    def reduce_codes(b):
        rows = pl.ds(pl.multiple_of(t * 32, 32), 32)
        s = cp[b, rows, :].astype(F32)
        for d in range(1, 8):
            scat[b, d].wait_recv()
            s = s + cr[b, d].astype(F32)
        s = s.astype(BF)
        cs[b] = s
        cf[b, rows, :] = s
        for d in range(1, 8):
            gath[b, d].start()

    def spread_codes(b):
        for d in range(1, 8):
            gath[b, d].wait_recv()
        packed = cf[b].astype(F32)
        turned = pltpu.roll(packed, 64, 1)
        both = jnp.concatenate([jnp.where(lowh, packed, turned), jnp.where(lowh, turned, packed)], axis=0)
        ids = idc[b]
        for g in range(16):
            xs[b, :, g * 128 : g * 128 + 128] = jnp.where(ids == lane_adapter(g), both, 0.0).astype(BF)

    outs = {}
    es, bgs = [e0, e1], [bg0, bg1]
    for n in range(2):
        for m in range(2):
            rows, ha, hb = slice(m * 256, m * 256 + 256), slice(m * 256, m * 256 + 128), slice(m * 256 + 128, m * 256 + 256)
            outs["or", n, m] = net.copy(es[n].at[3, ha], ol.at[n, ha], yr)
            outs["ol", n, m] = net.copy(es[n].at[3, hb], orr.at[n, hb], yl)
            outs["r", n, m] = net.copy(eR.at[n, rows], dl.at[n, rows], yr)
            outs["l", n, m] = net.copy(eL.at[n, rows], dr.at[n, rows], yl)

    def expand(n, b):
        for m in range(2):
            rows = slice(m * 256, m * 256 + 256)
            w = jnp.reshape(bgs[n][...], (2048, 256))
            got = jnp.dot(xs[b, rows, :], w, preferred_element_type=F32)
            es[n][b, rows, :] = got.astype(BF)
            if b == 3:
                outs["or", n, m].start()
                outs["ol", n, m].start()

    def relay(n, m):
        ha, hb = slice(m * 256, m * 256 + 128), slice(m * 256 + 128, m * 256 + 256)
        e = es[n]
        outs["or", n, m].wait_recv()
        eR[n, ha, :] = e[2, ha, :] + ol[n, ha, :]
        eR[n, hb, :] = e[2, hb, :]
        outs["r", n, m].start()
        outs["ol", n, m].wait_recv()
        eL[n, ha, :] = e[1, ha, :]
        eL[n, hb, :] = e[1, hb, :] + orr[n, hb, :]
        outs["l", n, m].start()

    def finish(n, m):
        outs["r", n, m].wait_recv()
        outs["l", n, m].wait_recv()
        rows = slice(m * 256, m * 256 + 256)
        cols = slice(n * 256, n * 256 + 256)
        total = part[0, 0, rows, cols].astype(F32) + pr[0, rows, cols].astype(F32)
        total = total + f1l[rows, cols].astype(F32) + f3r[rows, cols].astype(F32)
        delta = es[n][0, rows, :].astype(F32) + dl[n, rows, :].astype(F32) + dr[n, rows, :].astype(F32)
        out_ref[m * 64 : m * 64 + 64, :, cols] = (total + delta).astype(BF).reshape(64, 4, 256)

    loaded("kv")
    steps = [(0, 0, 1), (0, 1, 1), (0, 0, 2), (0, 1, 2), (0, 0, 3), (0, 1, 3), (0, 0, 4), (0, 1, 4)]
    for m in range(4):
        for i in (2 * m, 2 * m + 1):
            attend_chunk(i * 64, q_ref, kp, vp, suf, fresh, pcol, lcol, att)
            if i >= 1:
                z_step(*steps[i - 1])
            if i == 4:
                z_first(1)
        feat["r", m].start()
        feat["l", m].start()
        if m == 0:
            loaded("wo")
        if m >= 1:
            base_two(m - 1)
            forward_features(m - 1)
        project(m)
        if m >= 1:
            base_one(m - 1)
    z_step(*steps[7])
    z_first(2)
    base_two(3)
    for n, d in enumerate(id_msgs):
        d.wait_recv()
        idc[n + 1] = row_columns(idn.at[n])
    forward_features(3)
    loaded("a")
    loaded("b")
    codes(0)
    scatter_codes(0)
    base_one(3)
    z_step(1, 0, 1)
    z_step(1, 1, 1)
    codes(1)
    scatter_codes(1)
    z_step(1, 0, 2)
    z_step(1, 1, 2)
    codes(2)
    scatter_codes(2)
    reduce_codes(0)
    z_step(2, 0, 1)
    z_step(2, 1, 1)
    reduce_codes(1)
    for m in range(4):
        feat["rr", m].wait_recv()
        feat["ll", m].wait_recv()
    codes(3)
    scatter_codes(3)
    z_step(1, 0, 3)
    z_step(1, 1, 3)
    reduce_codes(2)
    z_step(2, 0, 2)
    z_step(2, 1, 2)
    spread_codes(0)
    reduce_codes(3)
    spread_codes(1)
    z_step(1, 0, 4)
    z_step(1, 1, 4)
    spread_codes(2)
    z_step(2, 0, 3)
    z_step(2, 1, 3)
    spread_codes(3)
    expand(0, 3)
    expand(0, 2)
    expand(0, 1)
    relay(0, 0)
    relay(0, 1)
    z_step(2, 0, 4)
    z_step(2, 1, 4)
    expand(1, 3)
    expand(1, 2)
    expand(1, 1)
    relay(1, 0)
    relay(1, 1)
    expand(0, 0)
    expand(1, 0)
    for m in range(4):
        base["1r", m].wait_recv()
        base["1l", m].wait_recv()
    for n in range(2):
        for m in range(2):
            finish(n, m)
    for d in net.sent:
        d.wait_send()


def local(
    queries,
    shared_prefix_cache,
    rollout_suffix_cache,
    fresh_key_value,
    rollout_prefix_index,
    rollout_suffix_length,
    rollout_adapter_index,
    output_projection_weight,
    adapter_shrink_weight,
    adapter_expand_weight,
):
    local_prefix = rollout_prefix_index - lax.axis_index("adapter") * 2
    vm, anyspec = pl.BlockSpec(memory_space=pltpu.VMEM), pl.BlockSpec(memory_space=pl.ANY)
    V = pltpu.VMEM
    return pl.pallas_call(
        mega_kernel,
        out_shape=jax.ShapeDtypeStruct((128, 4, 512), BF),
        in_specs=[vm, vm, vm, vm, anyspec, vm, vm, anyspec, anyspec, anyspec],
        out_specs=vm,
        scratch_shapes=[
            V((2048, 256), BF), V((2048, 256), BF), V((512, 128), F32), V((512, 128), F32),
            V((8, 512, 512), BF), V((8, 256, 512), BF), V((8, 256, 256), BF), V((8, 256, 256), BF),
            V((512, 512), BF), V((512, 512), BF), V((512, 512), BF), V((512, 512), BF),
            V((2, 4, 512, 512), BF), V((4, 512, 512), BF),
            V((512, 512), BF), V((512, 512), BF), V((512, 512), BF),
            V((512, 512), BF), V((512, 512), BF), V((512, 512), BF), V((512, 512), BF),
            V((3, 1, 128), jnp.int32), V((4, 512, 128), F32), V((512, 128), F32),
            V((4, 256, 128), BF), V((4, 8, 32, 128), BF), V((4, 32, 128), BF), V((4, 256, 128), BF),
            V((4, 512, 2048), BF),
            V((4, 512, 256), BF), V((4, 512, 256), BF), V((2, 512, 256), BF), V((2, 512, 256), BF),
            V((2, 512, 256), BF), V((2, 512, 256), BF), V((2, 512, 256), BF), V((2, 512, 256), BF),
            pltpu.SemaphoreType.DMA((16,)),
            pltpu.SemaphoreType.DMA((NMSG,)),
            pltpu.SemaphoreType.DMA((NMSG,)),
        ],
        compiler_params=pltpu.CompilerParams(
            vmem_limit_bytes=62 << 20, collective_id=0, has_side_effects=True
        ),
        cost_estimate=pl.CostEstimate(flops=16 * 10**9, bytes_accessed=12 * 10**6, transcendentals=4 * 10**6),
    )(
        local_prefix.reshape(1, 128),
        rollout_suffix_length.reshape(1, 128),
        rollout_adapter_index.reshape(1, 128),
        queries,
        shared_prefix_cache,
        rollout_suffix_cache.reshape(2, 4096, HEAD),
        fresh_key_value,
        output_projection_weight,
        adapter_shrink_weight.reshape(256, 512),
        adapter_expand_weight.reshape(256, 512),
    )


def solution(mesh):
    placed = (
        P("adapter", None, "tensor"),
        P(None, "adapter", None, "tensor"),
        P(None, "adapter", None, "tensor"),
        P(None, "adapter", None, "tensor"),
        P("adapter"),
        P("adapter"),
        P("adapter", None),
        P("tensor", None),
        P("adapter", None, "tensor"),
        P("adapter", None, "tensor"),
    )
    return jax.shard_map(
        local, mesh=mesh, in_specs=placed, out_specs=P("adapter", None, "tensor"), check_vma=False
    )
```

```python
import math
import jax
import jax.numpy as jnp
from jax import lax
from jax.experimental import pallas as pl
from jax.experimental.pallas import tpu as pltpu
from jax.sharding import PartitionSpec as P

HEAD = 128
NT = (((1,), (1,)), ((), ()))
F32 = jnp.float32
BF = jnp.bfloat16


def row_columns(row_ref):
    values = row_ref[...].astype(F32).astype(BF)
    pick = lax.broadcasted_iota(jnp.int32, (512, 128), 0) // 4 == lax.broadcasted_iota(
        jnp.int32, (512, 128), 1
    )
    spread = jnp.where(pick, jnp.broadcast_to(values.astype(F32), (512, 128)), 0.0).astype(BF)
    return jnp.dot(spread, jnp.ones((128, 128), BF), preferred_element_type=F32)


def attend_chunk(base, q_ref, kp, vp, suf, fresh, pcol, lcol, out_ref):
    factor = (HEAD ** -0.5) * math.log2(math.e)
    subs = []
    for sub in range(2):
        row = base + sub * 32
        for h in range(4):
            subs.append(q_ref[row // 4 : row // 4 + 8, :, h * HEAD : (h + 1) * HEAD].reshape(32, HEAD))
    q = jnp.concatenate(subs, axis=0)
    pc = jnp.concatenate(
        [pcol[base + sub * 32 : base + sub * 32 + 32, :] for sub in range(2) for h in range(4)], axis=0
    )
    second = pc > 0.5
    zero = jnp.zeros_like(q)
    wide = jnp.concatenate([jnp.where(second, zero, q), jnp.where(second, q, zero)], axis=1)
    scores = lax.dot_general(wide, kp[...], NT, preferred_element_type=F32)
    top = jnp.max(scores, axis=1, keepdims=True)
    rows_i = lax.broadcasted_iota(jnp.int32, (128, 256), 0)
    keys_i = lax.broadcasted_iota(jnp.int32, (128, 256), 1)
    same = (rows_i % 32) // 4 == keys_i // 32
    kpos = (keys_i % 32).astype(F32)
    rows_f = lax.broadcasted_iota(jnp.int32, (128, 32), 0)
    keys_f = lax.broadcasted_iota(jnp.int32, (128, 32), 1)
    fmask = ((rows_f % 32) // 4 == keys_f // 4) & (keys_f % 4 <= rows_f % 4)
    suf_scores, fresh_scores = [], []
    for sub in range(2):
        r0 = (base + sub * 32) // 4
        qs = q[sub * 128 : (sub + 1) * 128]
        ks = suf[0, r0 * 32 : r0 * 32 + 256, :]
        s = lax.dot_general(qs, ks, NT, preferred_element_type=F32)
        lc = jnp.concatenate([lcol[base + sub * 32 : base + sub * 32 + 32, :]] * 4, axis=0)
        lc = jnp.concatenate([lc, lc], axis=1)
        suf_scores.append(jnp.where(same & (kpos < lc), s, -jnp.inf))
        kf = fresh[0, r0 : r0 + 8].reshape(32, HEAD)
        f = lax.dot_general(qs, kf, NT, preferred_element_type=F32)
        fresh_scores.append(jnp.where(fmask, f, -jnp.inf))
    ssc = jnp.concatenate(suf_scores, axis=0)
    fsc = jnp.concatenate(fresh_scores, axis=0)
    top = jnp.maximum(top, jnp.maximum(jnp.max(ssc, axis=1, keepdims=True), jnp.max(fsc, axis=1, keepdims=True)))
    p = jnp.exp2((scores - top) * factor)
    ps = jnp.exp2((ssc - top) * factor)
    pf = jnp.exp2((fsc - top) * factor)
    total = (
        jnp.sum(p, axis=1, keepdims=True)
        + jnp.sum(ps, axis=1, keepdims=True)
        + jnp.sum(pf, axis=1, keepdims=True)
    )
    both = jnp.dot(p.astype(BF), vp[...], preferred_element_type=F32)
    acc = jnp.where(second, both[:, HEAD:], both[:, :HEAD])
    psb, pfb = ps.astype(BF), pf.astype(BF)
    extra = []
    for sub in range(2):
        r0 = (base + sub * 32) // 4
        vs = suf[1, r0 * 32 : r0 * 32 + 256, :]
        vf = fresh[1, r0 : r0 + 8].reshape(32, HEAD)
        e = jnp.dot(psb[sub * 128 : (sub + 1) * 128], vs, preferred_element_type=F32)
        e = e + jnp.dot(pfb[sub * 128 : (sub + 1) * 128], vf, preferred_element_type=F32)
        extra.append(e)
    acc = acc + jnp.concatenate(extra, axis=0)
    acc = (acc * (1.0 / total)).astype(BF)
    for sub in range(2):
        for h in range(4):
            out_ref[base + sub * 32 : base + sub * 32 + 32, h * HEAD : (h + 1) * HEAD] = acc[
                sub * 128 + h * 32 : sub * 128 + h * 32 + 32
            ]


NMSG = 128
MESHID = pl.DeviceIdType.MESH


class Net:
    def __init__(self, ssem, rsem):
        self.ssem, self.rsem, self.sent, self.count = ssem, rsem, [], 0

    def copy(self, src, dst, device):
        i = self.count
        self.count += 1
        d = pltpu.make_async_remote_copy(
            src_ref=src,
            dst_ref=dst,
            send_sem=self.ssem.at[i],
            recv_sem=self.rsem.at[i],
            device_id=device,
            device_id_type=MESHID,
        )
        self.sent.append(d)
        return d


def mega_kernel(
    pfx_ref, len_ref, idx_ref, q_hbm, prefix, suf_hbm, fresh_hbm, wo_hbm, a_hbm, b_hbm,
    out_ref,
    q_ref, suf, fresh, kp, vp, pcol, lcol, wo, ag, bg0, bg1, att, fl, fr, fo, part, pr, s1, s2, s3,
    t2l, t2r, f1l, f3r, idn, idc, acc, cp, cpr, cs, cx, ct, cf, xs, e0, e1, ol, orr, eR, eL, dl, dr,
    lsem, ssem, rsem,
):
    a, t = lax.axis_index("adapter"), lax.axis_index("tensor")
    z, y, x, c = a // 4, a % 4, t // 2, t % 2
    zr, zl = (((z + 1) % 8) * 4 + y, t), (((z + 7) % 8) * 4 + y, t)
    yr, yl, yo = (z * 4 + (y + 1) % 4, t), (z * 4 + (y + 3) % 4, t), (z * 4 + (y + 2) % 4, t)
    xr, xl, pc = (a, ((x + 1) % 4) * 2 + c), (a, ((x + 3) % 4) * 2 + c), (a, x * 2 + (1 - c))
    xo = (a, ((x + 2) % 4) * 2 + c)
    net = Net(ssem, rsem)

    barrier = pltpu.get_barrier_semaphore()
    everyone = [zr, zl, yr, yl, yo, xr, xl, xo, pc]
    for dev in everyone:
        pl.semaphore_signal(barrier, inc=1, device_id=dev, device_id_type=MESHID)

    loads, nl = {}, 0

    def load(name, src, dst):
        nonlocal nl
        d = pltpu.make_async_copy(src, dst, lsem.at[nl])
        nl += 1
        loads.setdefault(name, []).append(d)
        d.start()

    def loaded(name):
        for d in loads[name]:
            d.wait()

    load("kv", q_hbm, q_ref)
    load("kv", suf_hbm, suf)
    load("kv", fresh_hbm, fresh)
    for which, ref in enumerate((kp, vp)):
        for slot in range(2):
            load("kv", prefix.at[which, slot], ref.at[:, slot * HEAD : (slot + 1) * HEAD])
    load("a", a_hbm, ag.at[0])
    for j in range(8):
        dest = ((x + j % 4) % 4) * 2 + (c + j // 4) % 2
        load("wo", wo_hbm.at[:, pl.ds(pl.multiple_of(dest * 512, 512), 512)], wo.at[j])
    load("b", b_hbm.at[:, 0:256], bg0.at[0])
    load("b", b_hbm.at[:, 256:512], bg1.at[0])

    own = [a_hbm, b_hbm.at[:, 0:256], b_hbm.at[:, 256:512]]
    store = [ag, bg0, bg1]
    last = {(0, 0): 4, (0, 1): 3, (1, 0): 3, (1, 1): 4}
    hops = {}
    for mat in range(3):
        for h in range(2):
            rows = slice(h * 128, h * 128 + 128)
            for way in range(2):
                for k in range(1, last[(way, h)] + 1):
                    here = (8 - (k - 1)) % 8 if way == 0 else k - 1
                    there = (8 - k) % 8 if way == 0 else k
                    src = own[mat].at[rows] if k == 1 else store[mat].at[here, rows]
                    hops[mat, h, way, k] = net.copy(src, store[mat].at[there, rows], zr if way == 0 else zl)

    def z_first(mat):
        for h in range(2):
            for way in range(2):
                hops[mat, h, way, 1].start()

    def z_step(mat, h, k):
        for way in range(2):
            if k <= last[(way, h)]:
                hops[mat, h, way, k].wait_recv()
                if k < last[(way, h)]:
                    hops[mat, h, way, k + 1].start()

    id_msgs = [
        net.copy(idx_ref, idn.at[0], yr),
        net.copy(idx_ref, idn.at[1], yl),
        net.copy(idx_ref, idn.at[2], yo),
    ]

    feat = {}
    for m in range(4):
        rows, ha, hb = slice(m * 128, m * 128 + 128), slice(m * 128, m * 128 + 64), slice(m * 128 + 64, m * 128 + 128)
        feat["r", m] = net.copy(att.at[rows], fl.at[rows], yr)
        feat["l", m] = net.copy(att.at[rows], fr.at[rows], yl)
        feat["rr", m] = net.copy(fl.at[ha], fo.at[ha], yr)
        feat["ll", m] = net.copy(fr.at[hb], fo.at[hb], yl)
    base = {}
    for m in range(4):
        rows, ha, hb = slice(m * 128, m * 128 + 128), slice(m * 128, m * 128 + 64), slice(m * 128 + 64, m * 128 + 128)
        base["p", m] = net.copy(part.at[1, :, rows], pr.at[:, rows], pc)
        base["2r", m] = net.copy(s2.at[ha], t2l.at[ha], xr)
        base["2l", m] = net.copy(s2.at[hb], t2r.at[hb], xl)
        base["1r", m] = net.copy(s1.at[rows], f1l.at[rows], xr)
        base["1l", m] = net.copy(s3.at[rows], f3r.at[rows], xl)

    def project(m):
        rows = slice(m * 128, m * 128 + 128)
        here = att[rows, :]
        for j in (4, 5, 6, 7, 2, 1, 3, 0):
            got = jnp.dot(here, wo[j], preferred_element_type=F32)
            part[j // 4, j % 4, rows, :] = got.astype(BF)
            if j == 7:
                base["p", m].start()

    def forward_features(m):
        feat["r", m].wait_recv()
        feat["rr", m].start()
        feat["l", m].wait_recv()
        feat["ll", m].start()

    def paired(dx, rows):
        return part[0, dx, rows, :].astype(F32) + pr[dx, rows, :].astype(F32)

    def base_two(m):
        base["p", m].wait_recv()
        rows = slice(m * 128, m * 128 + 128)
        s2[rows, :] = paired(2, rows).astype(BF)
        base["2r", m].start()
        base["2l", m].start()

    def base_one(m):
        ha, hb = slice(m * 128, m * 128 + 64), slice(m * 128 + 64, m * 128 + 128)
        base["2r", m].wait_recv()
        s1[ha, :] = (paired(1, ha) + t2l[ha, :].astype(F32)).astype(BF)
        s1[hb, :] = paired(1, hb).astype(BF)
        base["1r", m].start()
        base["2l", m].wait_recv()
        s3[ha, :] = paired(3, ha).astype(BF)
        s3[hb, :] = (paired(3, hb) + t2r[hb, :].astype(F32)).astype(BF)
        base["1l", m].start()

    feats = [att, fl, fr, fo]
    low = lax.broadcasted_iota(jnp.int32, (512, 128), 1) < 64
    lowh = lax.broadcasted_iota(jnp.int32, (256, 128), 1) < 64

    def lane_adapter(g):
        first = ((z + g // 2) % 8) * 16 + y * 4 + (g % 2) * 2
        lanes = lax.broadcasted_iota(jnp.int32, (1, 128), 1) // 64
        return (lanes + first).astype(F32)

    def codes_part(b, slots, first=False):
        total = None if first else acc[b]
        ids = idc[b]
        for d in slots:
            got = lax.dot_general(feats[b][...], ag[d], NT, preferred_element_type=F32)
            for half in range(2):
                mine = jnp.where(ids == lane_adapter(2 * d + half), got[:, half * 128 : half * 128 + 128], 0.0)
                total = mine if total is None else total + mine
        acc[b] = total

    def codes_end(b):
        folded = acc[b] + pltpu.roll(acc[b], 64, 1)
        cp[b] = jnp.where(lowh, folded[:256], folded[256:]).astype(BF)
        pair_codes[b].start()

    mine = pl.ds(pl.multiple_of(c * 128, 128), 128)
    theirs = pl.ds(pl.multiple_of((1 - c) * 128, 128), 128)
    pair_codes = [net.copy(cp.at[b, theirs], cpr.at[b], pc) for b in range(4)]
    x_codes = [[net.copy(cs.at[b], cx.at[b, n], dev) for n, dev in enumerate((xr, xl, xo))] for b in range(4)]
    back_codes = [net.copy(ct.at[b], cf.at[b, mine], pc) for b in range(4)]

    def codes_pair(b):
        pair_codes[b].wait_recv()
        cs[b] = (cp[b, mine, :].astype(F32) + cpr[b].astype(F32)).astype(BF)
        for d in x_codes[b]:
            d.start()

    def codes_sum(b):
        s = cs[b].astype(F32)
        for n, d in enumerate(x_codes[b]):
            d.wait_recv()
            s = s + cx[b, n].astype(F32)
        s = s.astype(BF)
        ct[b] = s
        back_codes[b].start()
        cf[b, mine, :] = s

    def spread_codes(b):
        back_codes[b].wait_recv()
        packed = cf[b].astype(F32)
        turned = pltpu.roll(packed, 64, 1)
        both = jnp.concatenate([jnp.where(lowh, packed, turned), jnp.where(lowh, turned, packed)], axis=0)
        ids = idc[b]
        for g in range(16):
            xs[b, :, g * 128 : g * 128 + 128] = jnp.where(ids == lane_adapter(g), both, 0.0).astype(BF)

    outs = {}
    es, bgs = [e0, e1], [bg0, bg1]
    for n in range(2):
        for m in range(2):
            rows, ha, hb = slice(m * 256, m * 256 + 256), slice(m * 256, m * 256 + 128), slice(m * 256 + 128, m * 256 + 256)
            outs["or", n, m] = net.copy(es[n].at[3, ha], ol.at[n, ha], yr)
            outs["ol", n, m] = net.copy(es[n].at[3, hb], orr.at[n, hb], yl)
            outs["ra", n, m] = net.copy(eR.at[n, ha], dl.at[n, ha], yr)
            outs["rb", n, m] = net.copy(es[n].at[2, hb], dl.at[n, hb], yr)
            outs["la", n, m] = net.copy(es[n].at[1, ha], dr.at[n, ha], yl)
            outs["lb", n, m] = net.copy(eL.at[n, hb], dr.at[n, hb], yl)

    def expand(n, b):
        for m in range(2):
            rows = slice(m * 256, m * 256 + 256)
            w = jnp.reshape(bgs[n][...], (2048, 256))
            got = jnp.dot(xs[b, rows, :], w, preferred_element_type=F32)
            es[n][b, rows, :] = got.astype(BF)
            if b == 3:
                outs["or", n, m].start()
                outs["ol", n, m].start()
            if b == 2:
                outs["rb", n, m].start()
            if b == 1:
                outs["la", n, m].start()

    def relay(n, m):
        ha, hb = slice(m * 256, m * 256 + 128), slice(m * 256 + 128, m * 256 + 256)
        e = es[n]
        outs["or", n, m].wait_recv()
        eR[n, ha, :] = e[2, ha, :] + ol[n, ha, :]
        outs["ra", n, m].start()
        outs["ol", n, m].wait_recv()
        eL[n, hb, :] = e[1, hb, :] + orr[n, hb, :]
        outs["lb", n, m].start()

    def finish(n, m):
        for name in ("ra", "rb", "la", "lb"):
            outs[name, n, m].wait_recv()
        rows = slice(m * 256, m * 256 + 256)
        cols = slice(n * 256, n * 256 + 256)
        total = part[0, 0, rows, cols].astype(F32) + pr[0, rows, cols].astype(F32)
        total = total + f1l[rows, cols].astype(F32) + f3r[rows, cols].astype(F32)
        delta = es[n][0, rows, :].astype(F32) + dl[n, rows, :].astype(F32) + dr[n, rows, :].astype(F32)
        out_ref[m * 64 : m * 64 + 64, :, cols] = (total + delta).astype(BF).reshape(64, 4, 256)

    def attend(i):
        attend_chunk(i * 64, q_ref, kp, vp, suf, fresh, pcol, lcol, att)

    def send_features(m):
        feat["r", m].start()
        feat["l", m].start()

    def z_both(mat, k):
        z_step(mat, 0, k)
        z_step(mat, 1, k)

    pcol[...] = row_columns(pfx_ref) - (a * 2).astype(F32)
    lcol[...] = row_columns(len_ref)
    idc[0] = row_columns(idx_ref)
    loaded("kv")
    attend(0)
    pl.semaphore_wait(barrier, len(everyone))
    z_first(0)
    for d in id_msgs:
        d.start()
    attend(1)
    send_features(0)
    attend(2)
    attend(3)
    send_features(1)
    attend(4)
    z_step(0, 0, 1)
    attend(5)
    send_features(2)
    z_step(0, 1, 1)
    attend(6)
    forward_features(0)
    attend(7)
    send_features(3)
    z_step(0, 0, 2)
    loaded("wo")
    project(0)
    forward_features(1)
    z_step(0, 1, 2)
    project(1)
    forward_features(2)
    project(2)
    base_two(0)
    z_step(0, 0, 3)
    project(3)
    base_two(1)
    forward_features(3)
    z_step(0, 1, 3)
    z_first(1)
    for n, d in enumerate(id_msgs):
        d.wait_recv()
        idc[n + 1] = row_columns(idn.at[n])
    loaded("a")
    base_one(0)
    codes_part(0, (0, 1, 7, 2, 6), True)
    base_one(1)
    codes_part(1, (0, 1, 7, 2, 6), True)
    codes_part(2, (0, 1, 7, 2, 6), True)
    for b in range(3):
        codes_part(b, (3, 5))
    z_step(0, 0, 4)
    z_step(0, 1, 4)
    codes_part(0, (4,))
    codes_end(0)
    codes_part(1, (4,))
    codes_end(1)
    codes_pair(0)
    codes_part(2, (4,))
    codes_end(2)
    codes_pair(1)
    z_step(1, 0, 1)
    z_step(1, 1, 1)
    for m in range(4):
        feat["rr", m].wait_recv()
        feat["ll", m].wait_recv()
    codes_pair(2)
    codes_part(3, (0, 1, 7, 2, 6, 3, 5, 4), True)
    codes_end(3)
    codes_sum(0)
    codes_pair(3)
    base_two(2)
    base_two(3)
    codes_sum(1)
    z_both(1, 2)
    z_first(2)
    codes_sum(2)
    loaded("b")
    spread_codes(0)
    spread_codes(1)
    codes_sum(3)
    z_step(1, 0, 3)
    spread_codes(2)
    z_step(1, 1, 3)
    z_both(2, 1)
    base_one(2)
    spread_codes(3)
    base_one(3)
    z_both(1, 4)
    expand(0, 3)
    z_both(2, 2)
    expand(0, 2)
    expand(0, 1)
    z_both(2, 3)
    relay(0, 0)
    relay(0, 1)
    expand(0, 0)
    for m in range(4):
        base["1r", m].wait_recv()
        base["1l", m].wait_recv()
    z_both(2, 4)
    expand(1, 3)
    expand(1, 2)
    expand(1, 1)
    finish(0, 0)
    finish(0, 1)
    relay(1, 0)
    relay(1, 1)
    expand(1, 0)
    finish(1, 0)
    finish(1, 1)
    for d in net.sent:
        d.wait_send()


def local(
    queries,
    shared_prefix_cache,
    rollout_suffix_cache,
    fresh_key_value,
    rollout_prefix_index,
    rollout_suffix_length,
    rollout_adapter_index,
    output_projection_weight,
    adapter_shrink_weight,
    adapter_expand_weight,
):
    vm, anyspec = pl.BlockSpec(memory_space=pltpu.VMEM), pl.BlockSpec(memory_space=pl.ANY)
    V = pltpu.VMEM
    return pl.pallas_call(
        mega_kernel,
        out_shape=jax.ShapeDtypeStruct((128, 4, 512), BF),
        in_specs=[vm, vm, vm] + [anyspec] * 7,
        out_specs=vm,
        scratch_shapes=[
            V((128, 4, 512), BF), V((2, 4096, 128), BF), V((2, 128, 4, 128), BF),
            V((2048, 256), BF), V((2048, 256), BF), V((512, 128), F32), V((512, 128), F32),
            V((8, 512, 512), BF), V((8, 256, 512), BF), V((8, 256, 256), BF), V((8, 256, 256), BF),
            V((512, 512), BF), V((512, 512), BF), V((512, 512), BF), V((512, 512), BF),
            V((2, 4, 512, 512), BF), V((4, 512, 512), BF),
            V((512, 512), BF), V((512, 512), BF), V((512, 512), BF),
            V((512, 512), BF), V((512, 512), BF), V((512, 512), BF), V((512, 512), BF),
            V((3, 1, 128), jnp.int32), V((4, 512, 128), F32), V((4, 512, 128), F32),
            V((4, 256, 128), BF), V((4, 128, 128), BF), V((4, 128, 128), BF),
            V((4, 3, 128, 128), BF), V((4, 128, 128), BF), V((4, 256, 128), BF),
            V((4, 512, 2048), BF),
            V((4, 512, 256), BF), V((4, 512, 256), BF), V((2, 512, 256), BF), V((2, 512, 256), BF),
            V((2, 512, 256), BF), V((2, 512, 256), BF), V((2, 512, 256), BF), V((2, 512, 256), BF),
            pltpu.SemaphoreType.DMA((18,)),
            pltpu.SemaphoreType.DMA((NMSG,)),
            pltpu.SemaphoreType.DMA((NMSG,)),
        ],
        compiler_params=pltpu.CompilerParams(
            vmem_limit_bytes=62 << 20, collective_id=0, has_side_effects=True
        ),
        cost_estimate=pl.CostEstimate(flops=16 * 10**9, bytes_accessed=12 * 10**6, transcendentals=4 * 10**6),
    )(
        rollout_prefix_index.reshape(1, 128),
        rollout_suffix_length.reshape(1, 128),
        rollout_adapter_index.reshape(1, 128),
        queries,
        shared_prefix_cache,
        rollout_suffix_cache.reshape(2, 4096, HEAD),
        fresh_key_value,
        output_projection_weight,
        adapter_shrink_weight.reshape(256, 512),
        adapter_expand_weight.reshape(256, 512),
    )


def solution(mesh):
    placed = (
        P("adapter", None, "tensor"),
        P(None, "adapter", None, "tensor"),
        P(None, "adapter", None, "tensor"),
        P(None, "adapter", None, "tensor"),
        P("adapter"),
        P("adapter"),
        P("adapter", None),
        P("tensor", None),
        P("adapter", None, "tensor"),
        P("adapter", None, "tensor"),
    )
    return jax.shard_map(
        local, mesh=mesh, in_specs=placed, out_specs=P("adapter", None, "tensor"), check_vma=False
    )
```

```python
import math
import jax
import jax.numpy as jnp
from jax import lax
from jax.experimental import pallas as pl
from jax.experimental.pallas import tpu as pltpu
from jax.sharding import PartitionSpec as P

HEAD = 128
NT = (((1,), (1,)), ((), ()))
F32 = jnp.float32
BF = jnp.bfloat16


def row_columns(row_ref):
    values = row_ref[...].astype(F32).astype(BF)
    pick = lax.broadcasted_iota(jnp.int32, (512, 128), 0) // 4 == lax.broadcasted_iota(
        jnp.int32, (512, 128), 1
    )
    spread = jnp.where(pick, jnp.broadcast_to(values.astype(F32), (512, 128)), 0.0).astype(BF)
    return jnp.dot(spread, jnp.ones((128, 128), BF), preferred_element_type=F32)


def attend_chunk(base, q_ref, kp, vp, suf, fresh, pcol, lcol, out_ref):
    factor = (HEAD ** -0.5) * math.log2(math.e)
    subs = []
    for sub in range(2):
        row = base + sub * 32
        for h in range(4):
            subs.append(q_ref[row // 4 : row // 4 + 8, :, h * HEAD : (h + 1) * HEAD].reshape(32, HEAD))
    q = jnp.concatenate(subs, axis=0)
    pc = jnp.concatenate(
        [pcol[base + sub * 32 : base + sub * 32 + 32, :] for sub in range(2) for h in range(4)], axis=0
    )
    second = pc > 0.5
    zero = jnp.zeros_like(q)
    wide = jnp.concatenate([jnp.where(second, zero, q), jnp.where(second, q, zero)], axis=1)
    scores = lax.dot_general(wide, kp[...], NT, preferred_element_type=F32)
    top = jnp.max(scores, axis=1, keepdims=True)
    rows_i = lax.broadcasted_iota(jnp.int32, (128, 256), 0)
    keys_i = lax.broadcasted_iota(jnp.int32, (128, 256), 1)
    same = (rows_i % 32) // 4 == keys_i // 32
    kpos = (keys_i % 32).astype(F32)
    rows_f = lax.broadcasted_iota(jnp.int32, (128, 32), 0)
    keys_f = lax.broadcasted_iota(jnp.int32, (128, 32), 1)
    fmask = ((rows_f % 32) // 4 == keys_f // 4) & (keys_f % 4 <= rows_f % 4)
    suf_scores, fresh_scores = [], []
    for sub in range(2):
        r0 = (base + sub * 32) // 4
        qs = q[sub * 128 : (sub + 1) * 128]
        ks = suf[0, r0 * 32 : r0 * 32 + 256, :]
        s = lax.dot_general(qs, ks, NT, preferred_element_type=F32)
        lc = jnp.concatenate([lcol[base + sub * 32 : base + sub * 32 + 32, :]] * 4, axis=0)
        lc = jnp.concatenate([lc, lc], axis=1)
        suf_scores.append(jnp.where(same & (kpos < lc), s, -jnp.inf))
        kf = fresh[0, r0 : r0 + 8].reshape(32, HEAD)
        f = lax.dot_general(qs, kf, NT, preferred_element_type=F32)
        fresh_scores.append(jnp.where(fmask, f, -jnp.inf))
    ssc = jnp.concatenate(suf_scores, axis=0)
    fsc = jnp.concatenate(fresh_scores, axis=0)
    top = jnp.maximum(top, jnp.maximum(jnp.max(ssc, axis=1, keepdims=True), jnp.max(fsc, axis=1, keepdims=True)))
    p = jnp.exp2((scores - top) * factor)
    ps = jnp.exp2((ssc - top) * factor)
    pf = jnp.exp2((fsc - top) * factor)
    total = (
        jnp.sum(p, axis=1, keepdims=True)
        + jnp.sum(ps, axis=1, keepdims=True)
        + jnp.sum(pf, axis=1, keepdims=True)
    )
    both = jnp.dot(p.astype(BF), vp[...], preferred_element_type=F32)
    acc = jnp.where(second, both[:, HEAD:], both[:, :HEAD])
    psb, pfb = ps.astype(BF), pf.astype(BF)
    extra = []
    for sub in range(2):
        r0 = (base + sub * 32) // 4
        vs = suf[1, r0 * 32 : r0 * 32 + 256, :]
        vf = fresh[1, r0 : r0 + 8].reshape(32, HEAD)
        e = jnp.dot(psb[sub * 128 : (sub + 1) * 128], vs, preferred_element_type=F32)
        e = e + jnp.dot(pfb[sub * 128 : (sub + 1) * 128], vf, preferred_element_type=F32)
        extra.append(e)
    acc = acc + jnp.concatenate(extra, axis=0)
    acc = (acc * (1.0 / total)).astype(BF)
    for sub in range(2):
        for h in range(4):
            out_ref[base + sub * 32 : base + sub * 32 + 32, h * HEAD : (h + 1) * HEAD] = acc[
                sub * 128 + h * 32 : sub * 128 + h * 32 + 32
            ]


NMSG = 128
MESHID = pl.DeviceIdType.MESH


class Net:
    def __init__(self, ssem, rsem):
        self.ssem, self.rsem, self.sent, self.count = ssem, rsem, [], 0

    def copy(self, src, dst, device):
        i = self.count
        self.count += 1
        d = pltpu.make_async_remote_copy(
            src_ref=src,
            dst_ref=dst,
            send_sem=self.ssem.at[i],
            recv_sem=self.rsem.at[i],
            device_id=device,
            device_id_type=MESHID,
        )
        self.sent.append(d)
        return d


def mega_kernel(
    pfx_ref, len_ref, idx_ref, q_hbm, prefix, suf_hbm, fresh_hbm, wo_hbm, a_hbm, b_hbm,
    out_ref,
    q_ref, suf, fresh, kp, vp, pcol, lcol, wo, ag, bg0, bg1, att, fl, fr, fo, part, pr, s1, s2, s3,
    t2l, t2r, f1l, f3r, idn, idc, acc, cp, cpr, cs, cx, ct, cf, xs, e0, e1, ol, orr, eR, eL, dl, dr,
    lsem, ssem, rsem,
):
    a, t = lax.axis_index("adapter"), lax.axis_index("tensor")
    z, y, x, c = a // 4, a % 4, t // 2, t % 2
    zr, zl = (((z + 1) % 8) * 4 + y, t), (((z + 7) % 8) * 4 + y, t)
    yr, yl, yo = (z * 4 + (y + 1) % 4, t), (z * 4 + (y + 3) % 4, t), (z * 4 + (y + 2) % 4, t)
    xr, xl, pc = (a, ((x + 1) % 4) * 2 + c), (a, ((x + 3) % 4) * 2 + c), (a, x * 2 + (1 - c))
    xo = (a, ((x + 2) % 4) * 2 + c)
    net = Net(ssem, rsem)

    barrier = pltpu.get_barrier_semaphore()
    everyone = [zr, zl, yr, yl, yo, xr, xl, xo, pc]
    for dev in everyone:
        pl.semaphore_signal(barrier, inc=1, device_id=dev, device_id_type=MESHID)

    loads, nl = {}, 0

    def load(name, src, dst):
        nonlocal nl
        d = pltpu.make_async_copy(src, dst, lsem.at[nl])
        nl += 1
        loads.setdefault(name, []).append(d)
        d.start()

    def loaded(name):
        for d in loads[name]:
            d.wait()

    load("kv", q_hbm, q_ref)
    load("kv", suf_hbm, suf)
    load("kv", fresh_hbm, fresh)
    for which, ref in enumerate((kp, vp)):
        for slot in range(2):
            load("kv", prefix.at[which, slot], ref.at[:, slot * HEAD : (slot + 1) * HEAD])
    load("a", a_hbm, ag.at[0])
    for j in range(8):
        dest = ((x + j % 4) % 4) * 2 + (c + j // 4) % 2
        load("wo", wo_hbm.at[:, pl.ds(pl.multiple_of(dest * 512, 512), 512)], wo.at[j])
    load("b", b_hbm.at[:, 0:256], bg0.at[0])
    load("b", b_hbm.at[:, 256:512], bg1.at[0])

    own = [a_hbm, b_hbm.at[:, 0:256], b_hbm.at[:, 256:512]]
    store = [ag, bg0, bg1]
    last = {(0, 0): 4, (0, 1): 3, (1, 0): 3, (1, 1): 4}
    hops = {}
    for mat in range(3):
        for h in range(2):
            rows = slice(h * 128, h * 128 + 128)
            for way in range(2):
                for k in range(1, last[(way, h)] + 1):
                    here = (8 - (k - 1)) % 8 if way == 0 else k - 1
                    there = (8 - k) % 8 if way == 0 else k
                    src = own[mat].at[rows] if k == 1 else store[mat].at[here, rows]
                    hops[mat, h, way, k] = net.copy(src, store[mat].at[there, rows], zr if way == 0 else zl)

    def z_first(mat):
        for h in range(2):
            for way in range(2):
                hops[mat, h, way, 1].start()

    def z_step(mat, h, k):
        for way in range(2):
            if k <= last[(way, h)]:
                hops[mat, h, way, k].wait_recv()
                if k < last[(way, h)]:
                    hops[mat, h, way, k + 1].start()

    id_msgs = [
        net.copy(idx_ref, idn.at[0], yr),
        net.copy(idx_ref, idn.at[1], yl),
        net.copy(idx_ref, idn.at[2], yo),
    ]

    feat = {}
    for m in range(4):
        rows, ha, hb = slice(m * 128, m * 128 + 128), slice(m * 128, m * 128 + 64), slice(m * 128 + 64, m * 128 + 128)
        feat["r", m] = net.copy(att.at[rows], fl.at[rows], yr)
        feat["l", m] = net.copy(att.at[rows], fr.at[rows], yl)
        feat["rr", m] = net.copy(fl.at[ha], fo.at[ha], yr)
        feat["ll", m] = net.copy(fr.at[hb], fo.at[hb], yl)
    base = {}
    for m in range(4):
        rows, ha, hb = slice(m * 128, m * 128 + 128), slice(m * 128, m * 128 + 64), slice(m * 128 + 64, m * 128 + 128)
        base["p", m] = net.copy(part.at[1, :, rows], pr.at[:, rows], pc)
        base["2r", m] = net.copy(s2.at[ha], t2l.at[ha], xr)
        base["2l", m] = net.copy(s2.at[hb], t2r.at[hb], xl)
        base["1r", m] = net.copy(s1.at[rows], f1l.at[rows], xr)
        base["1l", m] = net.copy(s3.at[rows], f3r.at[rows], xl)

    def project(m):
        rows = slice(m * 128, m * 128 + 128)
        here = att[rows, :]
        for j in (4, 5, 6, 7, 2, 1, 3, 0):
            got = jnp.dot(here, wo[j], preferred_element_type=F32)
            part[j // 4, j % 4, rows, :] = got.astype(BF)
            if j == 7:
                base["p", m].start()

    def forward_features(m):
        feat["r", m].wait_recv()
        feat["rr", m].start()
        feat["l", m].wait_recv()
        feat["ll", m].start()

    def paired(dx, rows):
        return part[0, dx, rows, :].astype(F32) + pr[dx, rows, :].astype(F32)

    def base_two(m):
        base["p", m].wait_recv()
        rows = slice(m * 128, m * 128 + 128)
        s2[rows, :] = paired(2, rows).astype(BF)
        base["2r", m].start()
        base["2l", m].start()

    def base_one(m):
        ha, hb = slice(m * 128, m * 128 + 64), slice(m * 128 + 64, m * 128 + 128)
        base["2r", m].wait_recv()
        s1[ha, :] = (paired(1, ha) + t2l[ha, :].astype(F32)).astype(BF)
        s1[hb, :] = paired(1, hb).astype(BF)
        base["1r", m].start()
        base["2l", m].wait_recv()
        s3[ha, :] = paired(3, ha).astype(BF)
        s3[hb, :] = (paired(3, hb) + t2r[hb, :].astype(F32)).astype(BF)
        base["1l", m].start()

    feats = [att, fl, fr, fo]
    low = lax.broadcasted_iota(jnp.int32, (512, 128), 1) < 64
    lowh = lax.broadcasted_iota(jnp.int32, (256, 128), 1) < 64

    def lane_adapter(g):
        first = ((z + g // 2) % 8) * 16 + y * 4 + (g % 2) * 2
        lanes = lax.broadcasted_iota(jnp.int32, (1, 128), 1) // 64
        return (lanes + first).astype(F32)

    def codes_part(b, slots, first=False):
        total = None if first else acc[b]
        ids = idc[b]
        for d in slots:
            got = lax.dot_general(feats[b][...], ag[d], NT, preferred_element_type=F32)
            for half in range(2):
                mine = jnp.where(ids == lane_adapter(2 * d + half), got[:, half * 128 : half * 128 + 128], 0.0)
                total = mine if total is None else total + mine
        acc[b] = total

    def codes_end(b):
        folded = acc[b] + pltpu.roll(acc[b], 64, 1)
        cp[b] = jnp.where(lowh, folded[:256], folded[256:]).astype(BF)
        pair_codes[b].start()

    mine = pl.ds(pl.multiple_of(c * 128, 128), 128)
    theirs = pl.ds(pl.multiple_of((1 - c) * 128, 128), 128)
    pair_codes = [net.copy(cp.at[b, theirs], cpr.at[b], pc) for b in range(4)]
    x_codes = [[net.copy(cs.at[b], cx.at[b, n], dev) for n, dev in enumerate((xr, xl, xo))] for b in range(4)]
    back_codes = [net.copy(ct.at[b], cf.at[b, mine], pc) for b in range(4)]

    def codes_pair(b):
        pair_codes[b].wait_recv()
        cs[b] = (cp[b, mine, :].astype(F32) + cpr[b].astype(F32)).astype(BF)
        for d in x_codes[b]:
            d.start()

    def codes_sum(b):
        s = cs[b].astype(F32)
        for n, d in enumerate(x_codes[b]):
            d.wait_recv()
            s = s + cx[b, n].astype(F32)
        s = s.astype(BF)
        ct[b] = s
        back_codes[b].start()
        cf[b, mine, :] = s

    def spread_codes(b):
        back_codes[b].wait_recv()
        packed = cf[b].astype(F32)
        turned = pltpu.roll(packed, 64, 1)
        both = jnp.concatenate([jnp.where(lowh, packed, turned), jnp.where(lowh, turned, packed)], axis=0)
        ids = idc[b]
        for g in range(16):
            xs[b, :, g * 128 : g * 128 + 128] = jnp.where(ids == lane_adapter(g), both, 0.0).astype(BF)

    outs = {}
    es, bgs = [e0, e1], [bg0, bg1]
    for n in range(2):
        for m in range(2):
            rows, ha, hb = slice(m * 256, m * 256 + 256), slice(m * 256, m * 256 + 128), slice(m * 256 + 128, m * 256 + 256)
            outs["or", n, m] = net.copy(es[n].at[3, ha], ol.at[n, ha], yr)
            outs["ol", n, m] = net.copy(es[n].at[3, hb], orr.at[n, hb], yl)
            outs["ra", n, m] = net.copy(eR.at[n, ha], dl.at[n, ha], yr)
            outs["rb", n, m] = net.copy(es[n].at[2, hb], dl.at[n, hb], yr)
            outs["la", n, m] = net.copy(es[n].at[1, ha], dr.at[n, ha], yl)
            outs["lb", n, m] = net.copy(eL.at[n, hb], dr.at[n, hb], yl)

    def expand(n, b):
        for m in range(2):
            rows = slice(m * 256, m * 256 + 256)
            w = jnp.reshape(bgs[n][...], (2048, 256))
            got = jnp.dot(xs[b, rows, :], w, preferred_element_type=F32)
            es[n][b, rows, :] = got.astype(BF)
            if b == 3:
                outs["or", n, m].start()
                outs["ol", n, m].start()
            if b == 2:
                outs["rb", n, m].start()
            if b == 1:
                outs["la", n, m].start()

    def relay(n, m):
        ha, hb = slice(m * 256, m * 256 + 128), slice(m * 256 + 128, m * 256 + 256)
        e = es[n]
        outs["or", n, m].wait_recv()
        eR[n, ha, :] = e[2, ha, :] + ol[n, ha, :]
        outs["ra", n, m].start()
        outs["ol", n, m].wait_recv()
        eL[n, hb, :] = e[1, hb, :] + orr[n, hb, :]
        outs["lb", n, m].start()

    def finish(n, m):
        for name in ("ra", "rb", "la", "lb"):
            outs[name, n, m].wait_recv()
        rows = slice(m * 256, m * 256 + 256)
        cols = slice(n * 256, n * 256 + 256)
        total = part[0, 0, rows, cols].astype(F32) + pr[0, rows, cols].astype(F32)
        total = total + f1l[rows, cols].astype(F32) + f3r[rows, cols].astype(F32)
        delta = es[n][0, rows, :].astype(F32) + dl[n, rows, :].astype(F32) + dr[n, rows, :].astype(F32)
        out_ref[rows, cols] = (total + delta).astype(BF)

    def attend(i):
        attend_chunk(i * 64, q_ref, kp, vp, suf, fresh, pcol, lcol, att)

    def send_features(m):
        feat["r", m].start()
        feat["l", m].start()

    def z_both(mat, k):
        z_step(mat, 0, k)
        z_step(mat, 1, k)

    pcol[...] = row_columns(pfx_ref) - (a * 2).astype(F32)
    lcol[...] = row_columns(len_ref)
    idc[0] = row_columns(idx_ref)
    loaded("kv")
    attend(0)
    pl.semaphore_wait(barrier, len(everyone))
    z_first(0)
    for d in id_msgs:
        d.start()
    attend(1)
    send_features(0)
    attend(2)
    attend(3)
    send_features(1)
    attend(4)
    z_step(0, 0, 1)
    attend(5)
    send_features(2)
    z_step(0, 1, 1)
    attend(6)
    forward_features(0)
    attend(7)
    send_features(3)
    z_step(0, 0, 2)
    loaded("wo")
    project(0)
    forward_features(1)
    z_step(0, 1, 2)
    project(1)
    forward_features(2)
    project(2)
    base_two(0)
    z_step(0, 0, 3)
    project(3)
    base_two(1)
    forward_features(3)
    z_step(0, 1, 3)
    z_first(1)
    for n, d in enumerate(id_msgs):
        d.wait_recv()
        idc[n + 1] = row_columns(idn.at[n])
    loaded("a")
    base_one(0)
    codes_part(0, (0, 1, 7, 2, 6), True)
    base_one(1)
    codes_part(1, (0, 1, 7, 2, 6), True)
    codes_part(2, (0, 1, 7, 2, 6), True)
    for b in range(3):
        codes_part(b, (3, 5))
    z_step(0, 0, 4)
    z_step(0, 1, 4)
    z_step(1, 0, 1)
    codes_part(0, (4,))
    codes_end(0)
    codes_part(1, (4,))
    codes_end(1)
    codes_pair(0)
    z_step(1, 1, 1)
    codes_part(2, (4,))
    codes_end(2)
    codes_pair(1)
    for m in range(4):
        feat["rr", m].wait_recv()
        feat["ll", m].wait_recv()
    codes_pair(2)
    codes_part(3, (0, 1, 7, 2, 6, 3, 5, 4), True)
    codes_end(3)
    z_step(1, 0, 2)
    codes_sum(0)
    codes_pair(3)
    base_two(2)
    base_two(3)
    z_step(1, 1, 2)
    z_first(2)
    codes_sum(1)
    codes_sum(2)
    loaded("b")
    spread_codes(0)
    z_step(1, 0, 3)
    spread_codes(1)
    codes_sum(3)
    z_step(1, 1, 3)
    spread_codes(2)
    z_step(2, 0, 1)
    base_one(2)
    base_one(3)
    z_step(2, 1, 1)
    spread_codes(3)
    z_both(1, 4)
    expand(0, 3)
    z_step(2, 0, 2)
    expand(0, 2)
    z_step(2, 1, 2)
    expand(0, 1)
    relay(0, 0)
    z_step(2, 0, 3)
    relay(0, 1)
    z_step(2, 1, 3)
    expand(0, 0)
    for m in range(4):
        base["1r", m].wait_recv()
        base["1l", m].wait_recv()
    z_both(2, 4)
    expand(1, 3)
    expand(1, 2)
    expand(1, 1)
    finish(0, 0)
    finish(0, 1)
    relay(1, 0)
    relay(1, 1)
    expand(1, 0)
    finish(1, 0)
    finish(1, 1)
    for d in net.sent:
        d.wait_send()


def local(
    queries,
    shared_prefix_cache,
    rollout_suffix_cache,
    fresh_key_value,
    rollout_prefix_index,
    rollout_suffix_length,
    rollout_adapter_index,
    output_projection_weight,
    adapter_shrink_weight,
    adapter_expand_weight,
):
    vm, anyspec = pl.BlockSpec(memory_space=pltpu.VMEM), pl.BlockSpec(memory_space=pl.ANY)
    V = pltpu.VMEM
    return pl.pallas_call(
        mega_kernel,
        out_shape=jax.ShapeDtypeStruct((512, 512), BF),
        in_specs=[vm, vm, vm] + [anyspec] * 7,
        out_specs=vm,
        scratch_shapes=[
            V((128, 4, 512), BF), V((2, 4096, 128), BF), V((2, 128, 4, 128), BF),
            V((2048, 256), BF), V((2048, 256), BF), V((512, 128), F32), V((512, 128), F32),
            V((8, 512, 512), BF), V((8, 256, 512), BF), V((8, 256, 256), BF), V((8, 256, 256), BF),
            V((512, 512), BF), V((512, 512), BF), V((512, 512), BF), V((512, 512), BF),
            V((2, 4, 512, 512), BF), V((4, 512, 512), BF),
            V((512, 512), BF), V((512, 512), BF), V((512, 512), BF),
            V((512, 512), BF), V((512, 512), BF), V((512, 512), BF), V((512, 512), BF),
            V((3, 1, 128), jnp.int32), V((4, 512, 128), F32), V((4, 512, 128), F32),
            V((4, 256, 128), BF), V((4, 128, 128), BF), V((4, 128, 128), BF),
            V((4, 3, 128, 128), BF), V((4, 128, 128), BF), V((4, 256, 128), BF),
            V((4, 512, 2048), BF),
            V((4, 512, 256), BF), V((4, 512, 256), BF), V((2, 512, 256), BF), V((2, 512, 256), BF),
            V((2, 512, 256), BF), V((2, 512, 256), BF), V((2, 512, 256), BF), V((2, 512, 256), BF),
            pltpu.SemaphoreType.DMA((18,)),
            pltpu.SemaphoreType.DMA((NMSG,)),
            pltpu.SemaphoreType.DMA((NMSG,)),
        ],
        compiler_params=pltpu.CompilerParams(
            vmem_limit_bytes=62 << 20, collective_id=0, has_side_effects=True
        ),
        cost_estimate=pl.CostEstimate(flops=16 * 10**9, bytes_accessed=12 * 10**6, transcendentals=4 * 10**6),
    )(
        rollout_prefix_index.reshape(1, 128),
        rollout_suffix_length.reshape(1, 128),
        rollout_adapter_index.reshape(1, 128),
        queries,
        shared_prefix_cache,
        rollout_suffix_cache.reshape(2, 4096, HEAD),
        fresh_key_value,
        output_projection_weight,
        adapter_shrink_weight.reshape(256, 512),
        adapter_expand_weight.reshape(256, 512),
    ).reshape(128, 4, 512)


def solution(mesh):
    placed = (
        P("adapter", None, "tensor"),
        P(None, "adapter", None, "tensor"),
        P(None, "adapter", None, "tensor"),
        P(None, "adapter", None, "tensor"),
        P("adapter"),
        P("adapter"),
        P("adapter", None),
        P("tensor", None),
        P("adapter", None, "tensor"),
        P("adapter", None, "tensor"),
    )
    return jax.shard_map(
        local, mesh=mesh, in_specs=placed, out_specs=P("adapter", None, "tensor"), check_vma=False
    )
```
